32 devices in a mesh: edge: 8 (over z, y), chan: 4 (over x, core).
Axes of the slice: x: 2, y: 2, z: 4, core: 2. Of those that a mesh axis runs over, the one named last changes fastest.
Arguments:
- node_states: bfloat16 [128, 49, 256], P('edge', None, 'chan'), may hold values from -6 to 6
- edge_vectors: float32 [3, 4096], P(None, ('edge', 'chan')), may hold values from -5.6 to 5.6, as said below
- source_part: int32 [4096, 1], P('edge'), may hold values from 0 to 7; in each aligned block of 512 rows (0 to 511, 512 to 1023, ...) at most 128 rows name the same one
- source_slot: int32 [4096], P('edge'), may hold values from 0 to 15
- target_slot: int32 [4096], P('edge'), may hold values from 0 to 15
- live_edges: int32 [8], P('edge'), may hold values from 1 to 512, 3072 in all
- weight_zero: bfloat16 [7, 256, 7, 256], P(None, 'chan'), may hold values from -0.125 to 0.125
- weight_one: bfloat16 [2, 6, 256, 6, 256], P(None, None, 'chan'), may hold values from -0.109375 to 0.109375
- weight_two: bfloat16 [2, 5, 256, 5, 256], P(None, None, 'chan'), may hold values from -0.125 to 0.125
Outputs:
- aggregated: bfloat16 [128, 49, 256], P('edge', None, 'chan')
The draws below stay inside these ranges and needn't reach their ends.
Inputs may be any that keep to these rules, and one draw needn't show every extreme that they name: `source_part`: in each aligned block of 512 rows (the edges of one partition's slab) no partition number appears more than 128 times, and some number appears exactly 128 times. Edges are grouped by destination partition: the destination of an edge in slab p is node p * 16 + target_slot. `live_edges`: live slots stand at the front of each slab; the fullest slab is full. `edge_vectors`: every column has length between 0.8 and 5.6.
All inputs are finite; a program needn't handle non-finite values. No bound on the sum of `live_edges` on one device may be relied on, other than what follows from the above.
Results may differ from the reference program's by a relative error of at most 0.015.
Values may be sent and summed in bfloat16 or wider, within the bound.
A program may use at most 128 MiB of HBM per device.

```python
import math
import jax
import jax.numpy as jnp
import numpy as np
from jax import lax

C = 256
LMAX = 6
MMAX = 2
N_DEV = 16
E_CAP = 512
NODES = 128
EDGES = 4096
CAP = 128
COEFS = 49
KEPT = 29
N_EDGE = 8
N_CHAN = 4


def draw_edge_vectors(key, part):
    first_key, second_key = jax.random.split(jax.random.fold_in(key, 17))
    raw = jax.random.normal(first_key, (3, EDGES), jnp.float32)
    length = jax.random.uniform(second_key, (1, EDGES), jnp.float32, 0.8, 5.6)
    norm_value = jnp.sqrt(jnp.sum(raw * raw, axis=0, keepdims=True))
    direction = raw / jnp.maximum(norm_value, 1e-06)
    return jnp.clip(direction * length, -5.6, 5.6)


def with_ends(entries, rng, smallest, largest):
    index_at = [jax.random.randint(jax.random.fold_in(rng, axis), (), 0, length) for axis, length in enumerate(entries.shape)]
    longest = entries.shape.index(max(entries.shape))
    beside = index_at[:longest] + [(index_at[longest] + 1) % entries.shape[longest]] + index_at[longest + 1:]
    return entries.at[tuple(index_at)].set(smallest).at[tuple(beside)].set(largest)


def level_of(stream_key, shape, cuts, smallest, high):
    gain = 1.0
    for dim, shards_of in cuts:
        draws = jax.random.uniform(jax.random.fold_in(jax.random.fold_in(stream_key, 6), dim), (shards_of,), jnp.float32, smallest / len(cuts), high / len(cuts))
        gain = gain * jnp.repeat(jnp.exp(draws), shape[dim] // shards_of).reshape((-1,) + (1,) * (len(shape) - 1 - dim))
    return gain


def length_profile(number_of, total, bound, skew):
    portions = [(1 << 20) // math.isqrt(rank ** skew) + 1 for rank in range(2, number_of + 1)]
    spare, given = total - bound - (number_of - 1), [1] * (number_of - 1)
    while spare > 0:
        movable = [i for i in range(number_of - 1) if given[i] < bound]
        mass, budget = sum([portions[i] for i in movable]), spare
        for i in movable:
            more = min(bound - given[i], max(1, budget * portions[i] // mass), spare)
            given[i] = given[i] + more
            spare = spare - more
    return np.array([bound] + given)


def uneven_parts(stream_key, count, total, limit, lean):
    if count == 2:
        one = jax.random.randint(stream_key, (), max(1, total - limit), min(limit, total - 1) + 1)
        return jnp.stack([one, total - one])
    lengths = jnp.asarray(length_profile(count, total, limit, lean), jnp.int32)
    twos = (count - 1) // 2
    source_of, receiver = lengths[1:1 + 2 * twos:2], lengths[2:2 + 2 * twos:2]
    slack = jnp.minimum(source_of - 1, limit - receiver)
    passed = jax.random.randint(jax.random.fold_in(stream_key, 1), (twos,), 0, 1 << 20) % (slack + 1)
    lengths = lengths.at[1:1 + 2 * twos:2].set(source_of - passed).at[2:2 + 2 * twos:2].set(receiver + passed)
    return lengths[jax.random.permutation(jax.random.fold_in(stream_key, 2), count)]


def assign_block(own_key, own, number, rows, amount, top, most, lean):
    sequence = jax.random.permutation(own_key, amount)
    packed, usual = load_shares(amount, rows * top, most, lean, True), load_shares(amount, rows * top, most, lean, False)
    places = jnp.arange(amount)

    def named(sizes, turn):
        used = int((sizes > 0).sum())
        fixed = max(1, used // 4)
        passed = fixed + (places - fixed + turn * (used - fixed)) % max(1, amount - fixed)
        return jnp.zeros((amount,), jnp.int32).at[sequence[jnp.where(places < fixed, places, passed)]].set(jnp.asarray(sizes, jnp.int32))

    sizes = jnp.where(number % 4 == 0, named(packed, number // 4), named(usual, number - number // 4 - 1))
    mixed = jax.random.permutation(jax.random.fold_in(own, 3), amount)
    giver, receiver = mixed[0:amount // 2 * 2:2], mixed[1:amount // 2 * 2:2]
    room = jnp.minimum(sizes[giver] - 1, most - sizes[receiver]) // 2
    room = jnp.where((giver == sequence[0]) | (receiver == sequence[0]) | (sizes[receiver] == 0), 0, jnp.maximum(room, 0))
    passed = jax.random.randint(jax.random.fold_in(own, 4), (amount // 2,), 0, 1 << 20) % (room + 1)
    sizes = sizes.at[giver].add(-passed).at[receiver].add(passed)
    labels = jnp.searchsorted(jnp.cumsum(sizes), jnp.arange(rows * top), side="right").astype(jnp.int32)
    table = labels.reshape(top, rows).T
    table = table[jax.random.permutation(jax.random.fold_in(own, 1), rows)]
    turn = jax.random.randint(jax.random.fold_in(own, 2), (rows, 1), 0, top)
    return jnp.take_along_axis(table, (jnp.arange(top)[None, :] + turn) % top, axis=1)


def load_shares(count, total, bound, lean, full):
    loads = [(1 << 20) // math.isqrt(grade ** lean) + 1 for grade in range(1, count + 1)]
    largest = bound if full else min(bound, max(-(-total // count), total * loads[0] // sum(loads)))
    least = 1 if total - largest >= count - 1 else 0
    counts, rest = [largest] + [least] * (count - 1), total - largest - least * (count - 1)
    while rest > 0:
        movable = [i for i in range(1, count) if counts[i] < largest] or [i for i in range(1, count) if counts[i] < bound]
        mass, budget = sum([loads[i] for i in movable]), rest
        for i in movable:
            addition = min(bound - counts[i], max(1, budget * loads[i] // mass), rest)
            counts[i] = counts[i] + addition
            rest = rest - addition
    return np.array(counts)


def scatter_about(stream_key, shape, width, bound, cuts=(), kind=jnp.bfloat16):
    result = width * jax.random.normal(stream_key, shape, jnp.float32)
    if cuts:
        result = result * level_of(stream_key, shape, cuts, -0.22, 0.18)
    return jnp.clip(result, -bound, bound).astype(kind)


def setup_inputs(seed: int = 0) -> dict:
    splits = jax.random.split(jax.random.key(seed), 10)
    node_states = scatter_about(splits[0], (NODES, COEFS, C), 1.0, 6.0, ((0, 8), (2, 4)))
    edge_vectors = draw_edge_vectors(jax.random.fold_in(splits[9], 71), 0)
    source_part_keys = jax.random.split(jax.random.fold_in(splits[2], 1), EDGES // E_CAP)
    source_part_turns = jax.random.permutation(jax.random.fold_in(splits[2], 3), EDGES // E_CAP)
    source_part = jax.vmap(lambda own, number: assign_block(jax.random.fold_in(splits[2], 2), own, number, E_CAP, N_EDGE, 1, CAP, 2))(source_part_keys, source_part_turns).reshape((EDGES, 1))
    source_slot = with_ends(jax.random.randint(splits[3], (EDGES,), 0, N_DEV), jax.random.fold_in(splits[3], 1), 0, N_DEV - 1).astype(jnp.int32)
    target_slot = with_ends(jax.random.randint(splits[4], (EDGES,), 0, N_DEV), jax.random.fold_in(splits[4], 1), 0, N_DEV - 1).astype(jnp.int32)
    live_edges = uneven_parts(splits[5], N_EDGE, (3 * E_CAP * N_EDGE) // 4, E_CAP, 2).astype(jnp.int32)
    weight_zero = scatter_about(splits[6], (LMAX + 1, C, LMAX + 1, C), ((LMAX + 1) * C) ** -0.5, 0.125, ((1, 4),))
    weight_one = scatter_about(splits[7], (2, LMAX, C, LMAX, C), (2 * LMAX * C) ** -0.5, 0.109375, ((2, 4),))
    weight_two = scatter_about(splits[8], (2, LMAX - 1, C, LMAX - 1, C), (2 * (LMAX - 1) * C) ** -0.5, 0.125, ((2, 4),))
    return {"node_states": node_states, "edge_vectors": edge_vectors, "source_part": source_part, "source_slot": source_slot, "target_slot": target_slot, "live_edges": live_edges, "weight_zero": weight_zero, "weight_one": weight_one, "weight_two": weight_two}


cutoff_radius = 6.0
highest = lax.Precision.HIGHEST

def harmonics(coord_x, coord_y, coord_z, degree_top, order_top):
    results = {}
    real_part = [coord_x * 0.0 + 1.0]
    imag_part = [coord_x * 0.0]
    for azimuthal in range(1, order_top + 1):
        new_real = coord_x * real_part[-1] - coord_y * imag_part[-1]
        new_imag = coord_x * imag_part[-1] + coord_y * real_part[-1]
        real_part.append(new_real)
        imag_part.append(new_imag)
    for azimuthal in range(order_top + 1):
        start_value = (-1.0) ** azimuthal * math.prod(range(2 * azimuthal - 1, 0, -2))
        legendre = {azimuthal: coord_z * 0.0 + start_value}
        if azimuthal + 1 <= degree_top:
            legendre[azimuthal + 1] = coord_z * ((2 * azimuthal + 1) * start_value)
        for degree in range(azimuthal + 2, degree_top + 1):
            legendre[degree] = ((2 * degree - 1) * coord_z * legendre[degree - 1] - (degree + azimuthal - 1) * legendre[degree - 2]) / (degree - azimuthal)
        for degree in range(azimuthal, degree_top + 1):
            factor = math.sqrt((2 * degree + 1) / (4.0 * math.pi) * math.factorial(degree - azimuthal) / math.factorial(degree + azimuthal))
            if azimuthal == 0:
                results[degree, 0] = factor * legendre[degree]
            else:
                results[degree, azimuthal] = math.sqrt(2.0) * factor * legendre[degree] * real_part[azimuthal]
                results[degree, -azimuthal] = math.sqrt(2.0) * factor * legendre[degree] * imag_part[azimuthal]
    return results

def kept_rows():
    row_list = [(degree, 0) for degree in range(LMAX + 1)]
    for azimuthal in range(1, MMAX + 1):
        row_list += [(degree, azimuthal) for degree in range(azimuthal, LMAX + 1)]
        row_list += [(degree, -azimuthal) for degree in range(azimuthal, LMAX + 1)]
    return row_list

def invert_small(matrix):
    order_size = matrix.shape[0]
    work = np.concatenate([matrix, np.eye(order_size)], axis=1)
    for column in range(order_size):
        work[column] = work[column] / work[column, column]
        for row_index in range(order_size):
            if row_index != column:
                work[row_index] = work[row_index] - work[row_index, column] * work[column]
    return work[:, order_size:]

def sample_tables():
    sample_count = 2 * (LMAX + 1) ** 2
    positions = np.arange(sample_count) + 0.5
    height = 1.0 - 2.0 * positions / sample_count
    radius = np.sqrt(1.0 - height * height)
    azimuth = math.pi * (3.0 - math.sqrt(5.0)) * positions
    points = np.stack([radius * np.cos(azimuth), radius * np.sin(azimuth), height])
    values = harmonics(points[0], points[1], points[2], LMAX, LMAX)
    inverses = []
    for degree in range(LMAX + 1):
        sampled = np.stack([values[degree, azimuthal] for azimuthal in range(-degree, degree + 1)])
        inverses.append(sampled.T @ invert_small(sampled @ sampled.T))
    return (points, inverses)

def wigner_rows(vectors):
    length = jnp.sqrt(lax.optimization_barrier(jnp.sum(vectors * vectors, axis=0)))
    direction = vectors / length
    pick_first = jnp.where(jnp.abs(direction[0]) < 0.6, 1.0, 0.0).astype(jnp.float32)
    helper = jnp.stack([pick_first, 1.0 - pick_first, jnp.zeros_like(pick_first)])
    first_axis = jnp.cross(direction, helper, axis=0)
    first_axis = first_axis / jnp.sqrt(lax.optimization_barrier(jnp.sum(first_axis * first_axis, axis=0)))
    second_axis = jnp.cross(direction, first_axis, axis=0)
    frames = jnp.stack([first_axis, second_axis, direction])
    points, inverses = sample_tables()
    sample = jnp.asarray(points, jnp.float32)
    turned = jnp.einsum('rce,ck->rek', frames, sample, precision=highest)
    values = harmonics(turned[0], turned[1], turned[2], LMAX, MMAX)
    pieces = []
    for degree, azimuthal in kept_rows():
        table = jnp.asarray(inverses[degree], jnp.float32)
        pieces.append(jnp.dot(values[degree, azimuthal], table, precision=highest))
    compact = jnp.concatenate(pieces, axis=1)
    envelope = 0.5 * (jnp.cos(math.pi * length / cutoff_radius) + 1.0)
    return (compact, envelope)

def expand_rows(compact):
    padded_rows = []
    offset = 0
    for degree, azimuthal in kept_rows():
        span_size = 2 * degree + 1
        segment = compact[:, offset:offset + span_size]
        padded_rows.append(jnp.pad(segment, ((0, 0), (degree * degree, (LMAX + 1) ** 2 - degree * degree - span_size))))
        offset += span_size
    return jnp.stack(padded_rows, axis=1)

def convolve(turned, weight_zero, weight_one, weight_two, contract):
    end_zero = LMAX + 1
    end_one_plus = end_zero + LMAX
    end_one_minus = end_one_plus + LMAX
    end_two_plus = end_one_minus + LMAX - 1
    zero_part = turned[:end_zero]
    one_plus = turned[end_zero:end_one_plus]
    one_minus = turned[end_one_plus:end_one_minus]
    two_plus = turned[end_one_minus:end_two_plus]
    two_minus = turned[end_two_plus:]
    pattern = 'lce,lcjd->dje'
    out_zero = contract(pattern, zero_part, weight_zero)
    out_one_plus = contract(pattern, one_plus, weight_one[0]) - contract(pattern, one_minus, weight_one[1])
    out_one_minus = contract(pattern, one_minus, weight_one[0]) + contract(pattern, one_plus, weight_one[1])
    out_two_plus = contract(pattern, two_plus, weight_two[0]) - contract(pattern, two_minus, weight_two[1])
    out_two_minus = contract(pattern, two_minus, weight_two[0]) + contract(pattern, two_plus, weight_two[1])
    return jnp.concatenate([out_zero, out_one_plus, out_one_minus, out_two_plus, out_two_minus], axis=1)

def rounded(values):
    return lax.optimization_barrier(values.astype(jnp.bfloat16))

def float_contract(pattern, first_operand, second_operand):
    return jnp.einsum(pattern, first_operand.astype(jnp.float32), second_operand.astype(jnp.float32))

def reference(node_states, edge_vectors, source_part, source_slot, target_slot, live_edges, weight_zero, weight_one, weight_two):
    per_group = C // N_CHAN

    def one_slab(partition):
        first_edge = (partition * E_CAP).astype(jnp.int32)
        vectors = lax.dynamic_slice_in_dim(edge_vectors, first_edge, E_CAP, 1)
        compact, envelope = wigner_rows(vectors)
        rotation = expand_rows(rounded(compact))
        owner_part = lax.dynamic_slice_in_dim(source_part[:, 0], first_edge, E_CAP, 0)
        source_slots = lax.dynamic_slice_in_dim(source_slot, first_edge, E_CAP, 0)
        targets = lax.dynamic_slice_in_dim(target_slot, first_edge, E_CAP, 0)
        sources = node_states[owner_part * N_DEV + source_slots]
        turned = rounded(jnp.einsum('eik,ekc->ice', rotation.astype(jnp.float32), sources.astype(jnp.float32)))
        channel_mix = jnp.zeros((C, KEPT, E_CAP), jnp.float32)
        for group_index in range(N_CHAN):
            low_channel = group_index * per_group
            high_channel = low_channel + per_group
            partial_value = convolve(turned[:, low_channel:high_channel], weight_zero[:, low_channel:high_channel], weight_one[:, :, low_channel:high_channel], weight_two[:, :, low_channel:high_channel], float_contract)
            channel_mix = channel_mix + rounded(partial_value).astype(jnp.float32)
        alive_mask = (jnp.arange(E_CAP, dtype=jnp.int32) < live_edges[partition]).astype(jnp.float32)
        scaling = rounded(envelope).astype(jnp.float32) * alive_mask
        scaled = rounded(channel_mix * scaling)
        message = rounded(jnp.einsum('eik,cie->ekc', rotation.astype(jnp.float32), scaled.astype(jnp.float32)))
        selector = (jnp.arange(N_DEV, dtype=jnp.int32)[:, None] == targets[None, :]).astype(jnp.bfloat16)
        summed = jnp.dot(selector, message.reshape(E_CAP, COEFS * C), preferred_element_type=jnp.float32)
        return summed.astype(jnp.bfloat16).reshape(N_DEV, COEFS, C)
    blocks = lax.map(one_slab, jnp.arange(N_EDGE, dtype=jnp.int32))
    return blocks.reshape(NODES, COEFS, C)
```

```python
import math

import jax
import jax.numpy as jnp
import numpy as np
from jax import lax
from jax.experimental import pallas as pl
from jax.experimental.pallas import tpu as pltpu
from jax.sharding import PartitionSpec as P

LMAX = 6
MMAX = 2


cutoff_radius = 6.0
highest = lax.Precision.HIGHEST


def harmonics(coord_x, coord_y, coord_z, degree_top, order_top):
    results = {}
    real_part = [coord_x * 0.0 + 1.0]
    imag_part = [coord_x * 0.0]
    for azimuthal in range(1, order_top + 1):
        new_real = coord_x * real_part[-1] - coord_y * imag_part[-1]
        new_imag = coord_x * imag_part[-1] + coord_y * real_part[-1]
        real_part.append(new_real)
        imag_part.append(new_imag)
    for azimuthal in range(order_top + 1):
        start_value = (-1.0) ** azimuthal * math.prod(range(2 * azimuthal - 1, 0, -2))
        legendre = {azimuthal: coord_z * 0.0 + start_value}
        if azimuthal + 1 <= degree_top:
            legendre[azimuthal + 1] = coord_z * ((2 * azimuthal + 1) * start_value)
        for degree in range(azimuthal + 2, degree_top + 1):
            legendre[degree] = (
                (2 * degree - 1) * coord_z * legendre[degree - 1]
                - (degree + azimuthal - 1) * legendre[degree - 2]
            ) / (degree - azimuthal)
        for degree in range(azimuthal, degree_top + 1):
            factor = math.sqrt(
                (2 * degree + 1)
                / (4.0 * math.pi)
                * math.factorial(degree - azimuthal)
                / math.factorial(degree + azimuthal)
            )
            if azimuthal == 0:
                results[degree, 0] = factor * legendre[degree]
            else:
                results[degree, azimuthal] = (
                    math.sqrt(2.0) * factor * legendre[degree] * real_part[azimuthal]
                )
                results[degree, -azimuthal] = (
                    math.sqrt(2.0) * factor * legendre[degree] * imag_part[azimuthal]
                )
    return results


def kept_rows():
    row_list = [(degree, 0) for degree in range(LMAX + 1)]
    for azimuthal in range(1, MMAX + 1):
        row_list += [(degree, azimuthal) for degree in range(azimuthal, LMAX + 1)]
        row_list += [(degree, -azimuthal) for degree in range(azimuthal, LMAX + 1)]
    return row_list


def row_offsets():
    listing = []
    offset = 0
    for degree, azimuthal in kept_rows():
        listing.append((degree, offset))
        offset += 2 * degree + 1
    return listing


def invert_small(matrix):
    order_size = matrix.shape[0]
    work = np.concatenate([matrix, np.eye(order_size)], axis=1)
    for column in range(order_size):
        work[column] = work[column] / work[column, column]
        for row_index in range(order_size):
            if row_index != column:
                work[row_index] = work[row_index] - work[row_index, column] * work[column]
    return work[:, order_size:]


def sample_tables():
    sample_count = 2 * (LMAX + 1) ** 2
    positions = np.arange(sample_count) + 0.5
    height = 1.0 - 2.0 * positions / sample_count
    radius = np.sqrt(1.0 - height * height)
    azimuth = math.pi * (3.0 - math.sqrt(5.0)) * positions
    points = np.stack([radius * np.cos(azimuth), radius * np.sin(azimuth), height])
    values = harmonics(points[0], points[1], points[2], LMAX, LMAX)
    inverses = []
    for degree in range(LMAX + 1):
        sampled = np.stack([values[degree, azimuthal] for azimuthal in range(-degree, degree + 1)])
        inverses.append(sampled.T @ invert_small(sampled @ sampled.T))
    return (points, inverses)


def wigner_rows(vectors):
    length = jnp.sqrt(jnp.sum(vectors * vectors, axis=0))
    direction = vectors / length
    pick_first = jnp.where(jnp.abs(direction[0]) < 0.6, 1.0, 0.0).astype(jnp.float32)
    helper = jnp.stack([pick_first, 1.0 - pick_first, jnp.zeros_like(pick_first)])
    first_axis = jnp.cross(direction, helper, axis=0)
    first_axis = first_axis / jnp.sqrt(jnp.sum(first_axis * first_axis, axis=0))
    second_axis = jnp.cross(direction, first_axis, axis=0)
    frames = (first_axis, second_axis, direction)
    points, inverses = sample_tables()
    sample = jnp.asarray(points, jnp.float32)
    turned = [
        sum(sample[axis][:, None] * frame[axis][None, :] for axis in range(3)) for frame in frames
    ]
    values = harmonics(turned[0], turned[1], turned[2], LMAX, MMAX)
    edges = vectors.shape[1]
    pieces = {}
    for degree in range(LMAX + 1):
        orders = [row[1] for row in kept_rows() if row[0] == degree]
        stacked = jnp.concatenate([values[degree, order] for order in orders], axis=1)
        table = jnp.asarray(inverses[degree].T, jnp.float32)
        product = jnp.dot(table, stacked, precision=lax.Precision.HIGH)
        for index, order in enumerate(orders):
            pieces[degree, order] = product[:, index * edges : (index + 1) * edges]
    envelope = 0.5 * (jnp.cos(math.pi * length / cutoff_radius) + 1.0)
    return jnp.concatenate([pieces[row] for row in kept_rows()] + [envelope[None, :]], axis=0)


def rows_of(degree):
    return [
        (index, offset)
        for index, (row_degree, offset) in enumerate(row_offsets())
        if row_degree == degree
    ]


CHUNK = 32


def forward_kernel(compact_ref, sources_ref, turned_ref, rotation):
    rotation[...] = compact_ref[0].astype(jnp.float32)
    channels = sources_ref.shape[1]

    def body(step, carry):
        span = pl.ds(pl.multiple_of(step * CHUNK, CHUNK), CHUNK)
        for degree in range(LMAX + 1):
            listing = rows_of(degree)
            totals = [None] * len(listing)
            for inner in range(2 * degree + 1):
                value = sources_ref[degree * degree + inner, span, :].astype(jnp.float32)
                for place, (_, offset) in enumerate(listing):
                    at = offset + inner
                    term = rotation[at : at + 1, :] * value
                    totals[place] = term if totals[place] is None else totals[place] + term
            for place, (index, _) in enumerate(listing):
                turned_ref[index, span, :] = totals[place].astype(jnp.bfloat16)
        return carry

    lax.fori_loop(0, channels // CHUNK, body, 0)


def rotate_forward(compact, sources):
    blocks, rows, width = compact.shape
    coefs, channels, edges = sources.shape
    kept = len(kept_rows())
    return pl.pallas_call(
        forward_kernel,
        grid=(blocks,),
        in_specs=[
            pl.BlockSpec((1, rows, width), lambda b: (b, 0, 0)),
            pl.BlockSpec((coefs, channels, width), lambda b: (0, 0, b)),
        ],
        out_specs=pl.BlockSpec((kept, channels, width), lambda b: (0, 0, b)),
        out_shape=jax.ShapeDtypeStruct((kept, channels, edges), jnp.bfloat16),
        scratch_shapes=[pltpu.VMEM((rows, width), jnp.float32)],
        cost_estimate=pl.CostEstimate(
            flops=16_000_000, bytes_accessed=6_000_000, transcendentals=0
        ),
        name="rotate_forward",
    )(compact, sources)


def backward_kernel(starts, compact_ref, scaling_ref, *refs):
    count = len(starts)
    kept_refs, other_refs = refs[:count], refs[count : 2 * count]
    message_ref, rotation = refs[2 * count], refs[2 * count + 1]
    rotation[...] = compact_ref[0].astype(jnp.float32)
    channels = message_ref.shape[1]

    def body(step, carry):
        span = pl.ds(pl.multiple_of(step * CHUNK, CHUNK), CHUNK)
        scale = scaling_ref[0]
        for degree in range(LMAX + 1):
            values = []
            for index, offset in rows_of(degree):
                piece = max(p for p in range(count) if starts[p] <= index)
                row = index - starts[piece]
                mixed = kept_refs[piece][row, span, :].astype(jnp.float32) + other_refs[piece][
                    row, span, :
                ].astype(jnp.float32)
                values.append((mixed * scale, offset))
            for inner in range(2 * degree + 1):
                total = None
                for value, offset in values:
                    at = offset + inner
                    term = rotation[at : at + 1, :] * value
                    total = term if total is None else total + term
                message_ref[degree * degree + inner, span, :] = total.astype(jnp.bfloat16)
        return carry

    lax.fori_loop(0, channels // CHUNK, body, 0)


def rotate_back(compact, scaling, starts, kept, other):
    blocks, rows, width = compact.shape
    _, channels, edges = kept[0].shape
    coefs = (LMAX + 1) ** 2
    part_specs = [
        pl.BlockSpec((part.shape[0], channels, width), lambda b: (0, 0, b)) for part in kept
    ]

    def kernel(*refs):
        backward_kernel(starts, *refs)

    return pl.pallas_call(
        kernel,
        grid=(blocks,),
        in_specs=[
            pl.BlockSpec((1, rows, width), lambda b: (b, 0, 0)),
            pl.BlockSpec((1, 1, width), lambda b: (b, 0, 0)),
        ]
        + part_specs
        + part_specs,
        out_specs=pl.BlockSpec((coefs, channels, width), lambda b: (0, 0, b)),
        out_shape=jax.ShapeDtypeStruct((coefs, channels, edges), jnp.bfloat16),
        scratch_shapes=[pltpu.VMEM((rows, width), jnp.float32)],
        cost_estimate=pl.CostEstimate(
            flops=16_000_000, bytes_accessed=8_000_000, transcendentals=0
        ),
        name="rotate_back",
    )(compact, scaling, *kept, *other)


def mixed_contract(pattern, first_operand, second_operand):
    return jnp.einsum(pattern, first_operand, second_operand, preferred_element_type=jnp.float32)


def exchange(partial, group_count):
    rank = lax.axis_index("chan")
    rows, total, edges = partial.shape
    blocks = partial.reshape(rows, group_count, total // group_count, edges)

    def block(index):
        return lax.dynamic_index_in_dim(blocks, index, 1, keepdims=False)

    def swap(value, bit):
        return lax.ppermute(value, "chan", [(i, i ^ bit) for i in range(group_count)])

    def add(first, second):
        return (first.astype(jnp.float32) + second.astype(jnp.float32)).astype(jnp.bfloat16)

    far, near, far_near = rank ^ 2, rank ^ 1, rank ^ 3
    outgoing = add(block(far), swap(block(far_near), 1))
    arrived = swap(outgoing, 2)
    kept = add(block(rank), swap(block(near), 1))
    return kept, arrived


def one_hot(indices, width):
    return (indices[:, None] == jnp.arange(width, dtype=jnp.int32)[None, :]).astype(jnp.bfloat16)


def pick_columns(table, selector):
    picked = lax.dot_general(
        table, selector, (((0,), (1,)), ((), ())), preferred_element_type=jnp.float32
    )
    return picked.astype(jnp.bfloat16)


def shards(
    node_states,
    edge_vectors,
    source_part,
    source_slot,
    target_slot,
    live_edges,
    weight_zero,
    weight_one,
    weight_two,
):
    slab_size = source_slot.shape[0]
    local_nodes = node_states.shape[0]
    local_channels = node_states.shape[2]
    coef_count = node_states.shape[1]
    parts = lax.axis_size("edge")
    groups = lax.axis_size("chan")
    mine = lax.axis_index("edge")
    held = [node_states] + [
        lax.ppermute(node_states, "edge", [(i, (i + hop) % parts) for i in range(parts)])
        for hop in range(1, parts)
    ]
    everything = jnp.concatenate(held, axis=0)
    total_nodes = everything.shape[0]
    compact = lax.all_gather(
        wigner_rows(edge_vectors).astype(jnp.bfloat16), "chan", axis=0, tiled=False
    )
    distance = (mine - source_part[:, 0] + parts) % parts
    selector = one_hot(distance * local_nodes + source_slot, total_nodes)
    sources = pick_columns(
        everything.reshape(total_nodes, coef_count * local_channels), selector
    ).reshape(coef_count, local_channels, slab_size)
    turned = rotate_forward(compact, sources)
    sizes = [LMAX + 1, LMAX, LMAX, LMAX - 1, LMAX - 1]
    starts = [sum(sizes[:i]) for i in range(len(sizes))]
    zero, plus_one, minus_one, plus_two, minus_two = [
        turned[start : start + size] for start, size in zip(starts, sizes)
    ]
    pattern = "lce,lcjd->jde"

    def paired(plus, minus, weight):
        first = mixed_contract(pattern, plus, weight[0]) - mixed_contract(pattern, minus, weight[1])
        second = mixed_contract(pattern, minus, weight[0]) + mixed_contract(
            pattern, plus, weight[1]
        )
        return [first, second]

    partials = [mixed_contract(pattern, zero, weight_zero)]
    partials += paired(plus_one, minus_one, weight_one)
    partials += paired(plus_two, minus_two, weight_two)
    summed = [exchange(partial.astype(jnp.bfloat16), groups) for partial in partials]
    alive_mask = (jnp.arange(slab_size, dtype=jnp.int32) < live_edges[0]).astype(jnp.float32)
    envelope = compact[:, -1:, :].astype(jnp.float32)
    scaling = envelope * alive_mask.reshape(envelope.shape)
    message = rotate_back(
        compact, scaling, starts, [pair[0] for pair in summed], [pair[1] for pair in summed]
    ).reshape(coef_count * local_channels, slab_size)
    selector = (jnp.arange(local_nodes, dtype=jnp.int32)[:, None] == target_slot[None, :]).astype(
        jnp.bfloat16
    )
    summed = lax.dot_general(
        selector, message, (((1,), (1,)), ((), ())), preferred_element_type=jnp.float32
    )
    return summed.astype(jnp.bfloat16).reshape(local_nodes, coef_count, local_channels)


def solution(mesh):
    in_specs = (
        P("edge", None, "chan"),
        P(None, ("edge", "chan")),
        P("edge", None),
        P("edge"),
        P("edge"),
        P("edge"),
        P(None, "chan", None, None),
        P(None, None, "chan", None, None),
        P(None, None, "chan", None, None),
    )
    out_specs = P("edge", None, "chan")
    return jax.shard_map(shards, mesh=mesh, in_specs=in_specs, out_specs=out_specs, check_vma=False)
```

```python
import math

import jax
import jax.numpy as jnp
import numpy as np
from jax import lax
from jax.experimental import pallas as pl
from jax.experimental.pallas import tpu as pltpu
from jax.sharding import PartitionSpec as P

LMAX = 6
MMAX = 2


cutoff_radius = 6.0
highest = lax.Precision.HIGHEST


def harmonics(coord_x, coord_y, coord_z, degree_top, order_top):
    results = {}
    real_part = [coord_x * 0.0 + 1.0]
    imag_part = [coord_x * 0.0]
    for azimuthal in range(1, order_top + 1):
        new_real = coord_x * real_part[-1] - coord_y * imag_part[-1]
        new_imag = coord_x * imag_part[-1] + coord_y * real_part[-1]
        real_part.append(new_real)
        imag_part.append(new_imag)
    for azimuthal in range(order_top + 1):
        start_value = (-1.0) ** azimuthal * math.prod(range(2 * azimuthal - 1, 0, -2))
        legendre = {azimuthal: coord_z * 0.0 + start_value}
        if azimuthal + 1 <= degree_top:
            legendre[azimuthal + 1] = coord_z * ((2 * azimuthal + 1) * start_value)
        for degree in range(azimuthal + 2, degree_top + 1):
            legendre[degree] = (
                (2 * degree - 1) * coord_z * legendre[degree - 1]
                - (degree + azimuthal - 1) * legendre[degree - 2]
            ) / (degree - azimuthal)
        for degree in range(azimuthal, degree_top + 1):
            factor = math.sqrt(
                (2 * degree + 1)
                / (4.0 * math.pi)
                * math.factorial(degree - azimuthal)
                / math.factorial(degree + azimuthal)
            )
            if azimuthal == 0:
                results[degree, 0] = factor * legendre[degree]
            else:
                results[degree, azimuthal] = (
                    math.sqrt(2.0) * factor * legendre[degree] * real_part[azimuthal]
                )
                results[degree, -azimuthal] = (
                    math.sqrt(2.0) * factor * legendre[degree] * imag_part[azimuthal]
                )
    return results


def kept_rows():
    row_list = [(degree, 0) for degree in range(LMAX + 1)]
    for azimuthal in range(1, MMAX + 1):
        row_list += [(degree, azimuthal) for degree in range(azimuthal, LMAX + 1)]
        row_list += [(degree, -azimuthal) for degree in range(azimuthal, LMAX + 1)]
    return row_list


def padded_span(degree):
    return -(-(2 * degree + 1) // 8) * 8


def row_offsets():
    listing = []
    offset = 0
    for degree, azimuthal in kept_rows():
        listing.append((degree, offset))
        offset += padded_span(degree)
    return listing


def invert_small(matrix):
    order_size = matrix.shape[0]
    work = np.concatenate([matrix, np.eye(order_size)], axis=1)
    for column in range(order_size):
        work[column] = work[column] / work[column, column]
        for row_index in range(order_size):
            if row_index != column:
                work[row_index] = work[row_index] - work[row_index, column] * work[column]
    return work[:, order_size:]


def sample_tables():
    sample_count = 2 * (LMAX + 1) ** 2
    positions = np.arange(sample_count) + 0.5
    height = 1.0 - 2.0 * positions / sample_count
    radius = np.sqrt(1.0 - height * height)
    azimuth = math.pi * (3.0 - math.sqrt(5.0)) * positions
    points = np.stack([radius * np.cos(azimuth), radius * np.sin(azimuth), height])
    values = harmonics(points[0], points[1], points[2], LMAX, LMAX)
    inverses = []
    for degree in range(LMAX + 1):
        sampled = np.stack([values[degree, azimuthal] for azimuthal in range(-degree, degree + 1)])
        inverses.append(sampled.T @ invert_small(sampled @ sampled.T))
    return (points, inverses)


def wigner_rows(vectors):
    length = jnp.sqrt(jnp.sum(vectors * vectors, axis=0))
    direction = vectors / length
    pick_first = jnp.where(jnp.abs(direction[0]) < 0.6, 1.0, 0.0).astype(jnp.float32)
    helper = jnp.stack([pick_first, 1.0 - pick_first, jnp.zeros_like(pick_first)])
    first_axis = jnp.cross(direction, helper, axis=0)
    first_axis = first_axis / jnp.sqrt(jnp.sum(first_axis * first_axis, axis=0))
    second_axis = jnp.cross(direction, first_axis, axis=0)
    frames = (first_axis, second_axis, direction)
    points, inverses = sample_tables()
    sample = jnp.asarray(points, jnp.float32)
    turned = [
        sum(sample[axis][:, None] * frame[axis][None, :] for axis in range(3)) for frame in frames
    ]
    values = harmonics(turned[0], turned[1], turned[2], LMAX, MMAX)
    edges = vectors.shape[1]
    pieces = {}
    for degree in range(LMAX + 1):
        orders = [row[1] for row in kept_rows() if row[0] == degree]
        stacked = jnp.concatenate([values[degree, order] for order in orders], axis=1)
        span = 2 * degree + 1
        padding = ((0, padded_span(degree) - span), (0, 0))
        table = jnp.asarray(np.pad(inverses[degree].T, padding), jnp.float32)
        product = jnp.dot(table, stacked, precision=lax.Precision.HIGH)
        for index, order in enumerate(orders):
            pieces[degree, order] = product[:, index * edges : (index + 1) * edges]
    envelope = 0.5 * (jnp.cos(math.pi * length / cutoff_radius) + 1.0)
    fade = jnp.broadcast_to(envelope[None, :], (8, edges))
    return jnp.concatenate([pieces[row] for row in kept_rows()] + [fade], axis=0)


def rows_of(degree):
    return [
        (index, offset)
        for index, (row_degree, offset) in enumerate(row_offsets())
        if row_degree == degree
    ]


CHUNK = 32


def forward_kernel(compact_ref, sources_ref, turned_ref, rotation):
    rotation[...] = compact_ref[0].astype(jnp.float32)
    channels = sources_ref.shape[1]

    def body(step, carry):
        span = pl.ds(pl.multiple_of(step * CHUNK, CHUNK), CHUNK)
        for degree in range(LMAX + 1):
            listing = rows_of(degree)
            totals = [None] * len(listing)
            for inner in range(2 * degree + 1):
                value = sources_ref[degree * degree + inner, span, :].astype(jnp.float32)
                for place, (_, offset) in enumerate(listing):
                    at = offset + inner
                    term = rotation[at : at + 1, :] * value
                    totals[place] = term if totals[place] is None else totals[place] + term
            for place, (index, _) in enumerate(listing):
                turned_ref[index, span, :] = totals[place].astype(jnp.bfloat16)
        return carry

    lax.fori_loop(0, channels // CHUNK, body, 0)


def rotate_forward(compact, sources):
    blocks, rows, width = compact.shape
    coefs, channels, edges = sources.shape
    kept = len(kept_rows())
    return pl.pallas_call(
        forward_kernel,
        grid=(blocks,),
        in_specs=[
            pl.BlockSpec((1, rows, width), lambda b: (b, 0, 0)),
            pl.BlockSpec((coefs, channels, width), lambda b: (0, 0, b)),
        ],
        out_specs=pl.BlockSpec((kept, channels, width), lambda b: (0, 0, b)),
        out_shape=jax.ShapeDtypeStruct((kept, channels, edges), jnp.bfloat16),
        scratch_shapes=[pltpu.VMEM((rows, width), jnp.float32)],
        cost_estimate=pl.CostEstimate(
            flops=16_000_000, bytes_accessed=6_000_000, transcendentals=0
        ),
        name="rotate_forward",
    )(compact, sources)


def backward_kernel(starts, compact_ref, scaling_ref, *refs):
    count = len(starts)
    kept_refs, other_refs = refs[:count], refs[count : 2 * count]
    message_ref, rotation = refs[2 * count], refs[2 * count + 1]
    rotation[...] = compact_ref[0].astype(jnp.float32)
    channels = message_ref.shape[1]

    def body(step, carry):
        span = pl.ds(pl.multiple_of(step * CHUNK, CHUNK), CHUNK)
        scale = scaling_ref[0]
        for degree in range(LMAX + 1):
            values = []
            for index, offset in rows_of(degree):
                piece = max(p for p in range(count) if starts[p] <= index)
                row = index - starts[piece]
                mixed = kept_refs[piece][row, span, :].astype(jnp.float32) + other_refs[piece][
                    row, span, :
                ].astype(jnp.float32)
                values.append((mixed * scale, offset))
            for inner in range(2 * degree + 1):
                total = None
                for value, offset in values:
                    at = offset + inner
                    term = rotation[at : at + 1, :] * value
                    total = term if total is None else total + term
                message_ref[degree * degree + inner, span, :] = total.astype(jnp.bfloat16)
        return carry

    lax.fori_loop(0, channels // CHUNK, body, 0)


def rotate_back(compact, scaling, starts, kept, other):
    blocks, rows, width = compact.shape
    _, channels, edges = kept[0].shape
    coefs = (LMAX + 1) ** 2
    part_specs = [
        pl.BlockSpec((part.shape[0], channels, width), lambda b: (0, 0, b)) for part in kept
    ]

    def kernel(*refs):
        backward_kernel(starts, *refs)

    return pl.pallas_call(
        kernel,
        grid=(blocks,),
        in_specs=[
            pl.BlockSpec((1, rows, width), lambda b: (b, 0, 0)),
            pl.BlockSpec((1, 1, width), lambda b: (b, 0, 0)),
        ]
        + part_specs
        + part_specs,
        out_specs=pl.BlockSpec((coefs, channels, width), lambda b: (0, 0, b)),
        out_shape=jax.ShapeDtypeStruct((coefs, channels, edges), jnp.bfloat16),
        scratch_shapes=[pltpu.VMEM((rows, width), jnp.float32)],
        cost_estimate=pl.CostEstimate(
            flops=16_000_000, bytes_accessed=8_000_000, transcendentals=0
        ),
        name="rotate_back",
    )(compact, scaling, *kept, *other)


def mixed_contract(pattern, first_operand, second_operand):
    return jnp.einsum(pattern, first_operand, second_operand, preferred_element_type=jnp.float32)


def exchange(partial, group_count):
    rank = lax.axis_index("chan")
    rows, total, edges = partial.shape
    blocks = partial.reshape(rows, group_count, total // group_count, edges)

    def block(index):
        return lax.dynamic_index_in_dim(blocks, index, 1, keepdims=False)

    def swap(value, bit):
        return lax.ppermute(value, "chan", [(i, i ^ bit) for i in range(group_count)])

    def add(first, second):
        return (first.astype(jnp.float32) + second.astype(jnp.float32)).astype(jnp.bfloat16)

    far, near, far_near = rank ^ 2, rank ^ 1, rank ^ 3
    outgoing = add(block(far), swap(block(far_near), 1))
    arrived = swap(outgoing, 2)
    kept = add(block(rank), swap(block(near), 1))
    return kept, arrived


COEFS_PER_STEP = 7


def pick_kernel(index_ref, *refs):
    held_refs, sources_ref = refs[:-1], refs[-1]
    total_nodes = len(held_refs) * held_refs[0].shape[1]
    slab_size = index_ref.shape[1]
    rows = lax.broadcasted_iota(jnp.int32, (total_nodes, slab_size), 0)
    selector = jnp.where(rows == index_ref[...], 1.0, 0.0).astype(jnp.bfloat16)
    for coef in range(COEFS_PER_STEP):
        table = jnp.concatenate([ref[coef] for ref in held_refs], axis=0)
        picked = lax.dot_general(
            table, selector, (((0,), (0,)), ((), ())), preferred_element_type=jnp.float32
        )
        sources_ref[coef] = picked.astype(jnp.bfloat16)


def pick_sources(held, index):
    coefs, nodes, channels = held[0].shape
    slab_size = index.shape[1]
    return pl.pallas_call(
        pick_kernel,
        grid=(coefs // COEFS_PER_STEP,),
        in_specs=[pl.BlockSpec((1, slab_size), lambda k: (0, 0))]
        + [pl.BlockSpec((COEFS_PER_STEP, nodes, channels), lambda k: (k, 0, 0))] * len(held),
        out_specs=pl.BlockSpec((COEFS_PER_STEP, channels, slab_size), lambda k: (k, 0, 0)),
        out_shape=jax.ShapeDtypeStruct((coefs, channels, slab_size), jnp.bfloat16),
        cost_estimate=pl.CostEstimate(
            flops=400_000_000, bytes_accessed=5_000_000, transcendentals=0
        ),
        name="pick_sources",
    )(index, *held)


def shards(
    node_states,
    edge_vectors,
    source_part,
    source_slot,
    target_slot,
    live_edges,
    weight_zero,
    weight_one,
    weight_two,
):
    slab_size = source_slot.shape[0]
    local_nodes = node_states.shape[0]
    local_channels = node_states.shape[2]
    coef_count = node_states.shape[1]
    parts = lax.axis_size("edge")
    groups = lax.axis_size("chan")
    mine = lax.axis_index("edge")
    own = node_states.transpose(1, 0, 2)
    held = [own] + [
        lax.ppermute(own, "edge", [(i, (i + hop) % parts) for i in range(parts)])
        for hop in range(1, parts)
    ]
    compact = lax.all_gather(
        wigner_rows(edge_vectors).astype(jnp.bfloat16), "chan", axis=0, tiled=False
    )
    distance = (mine - source_part[:, 0] + parts) % parts
    sources = pick_sources(held, (distance * local_nodes + source_slot)[None, :])
    turned = rotate_forward(compact, sources)
    sizes = [LMAX + 1, LMAX, LMAX, LMAX - 1, LMAX - 1]
    starts = [sum(sizes[:i]) for i in range(len(sizes))]
    zero, plus_one, minus_one, plus_two, minus_two = [
        turned[start : start + size] for start, size in zip(starts, sizes)
    ]
    pattern = "lce,lcjd->jde"

    def paired(plus, minus, weight):
        first = mixed_contract(pattern, plus, weight[0]) - mixed_contract(pattern, minus, weight[1])
        second = mixed_contract(pattern, minus, weight[0]) + mixed_contract(
            pattern, plus, weight[1]
        )
        return [first, second]

    partials = [mixed_contract(pattern, zero, weight_zero)]
    partials += paired(plus_one, minus_one, weight_one)
    partials += paired(plus_two, minus_two, weight_two)
    summed = [exchange(partial.astype(jnp.bfloat16), groups) for partial in partials]
    alive_mask = (jnp.arange(slab_size, dtype=jnp.int32) < live_edges[0]).astype(jnp.float32)
    envelope = compact[:, -1:, :].astype(jnp.float32)
    scaling = envelope * alive_mask.reshape(envelope.shape)
    message = rotate_back(
        compact, scaling, starts, [pair[0] for pair in summed], [pair[1] for pair in summed]
    ).reshape(coef_count * local_channels, slab_size)
    selector = (jnp.arange(local_nodes, dtype=jnp.int32)[:, None] == target_slot[None, :]).astype(
        jnp.bfloat16
    )
    summed = lax.dot_general(
        selector, message, (((1,), (1,)), ((), ())), preferred_element_type=jnp.float32
    )
    return summed.astype(jnp.bfloat16).reshape(local_nodes, coef_count, local_channels)


def solution(mesh):
    in_specs = (
        P("edge", None, "chan"),
        P(None, ("edge", "chan")),
        P("edge", None),
        P("edge"),
        P("edge"),
        P("edge"),
        P(None, "chan", None, None),
        P(None, None, "chan", None, None),
        P(None, None, "chan", None, None),
    )
    out_specs = P("edge", None, "chan")
    return jax.shard_map(shards, mesh=mesh, in_specs=in_specs, out_specs=out_specs, check_vma=False)
```

```python
import math

import jax
import jax.numpy as jnp
import numpy as np
from jax import lax
from jax.experimental import pallas as pl
from jax.experimental.pallas import tpu as pltpu
from jax.sharding import PartitionSpec as P

LMAX = 6
MMAX = 2


cutoff_radius = 6.0
highest = lax.Precision.HIGHEST


def harmonics(coord_x, coord_y, coord_z, degree_top, order_top):
    results = {}
    real_part = [coord_x * 0.0 + 1.0]
    imag_part = [coord_x * 0.0]
    for azimuthal in range(1, order_top + 1):
        new_real = coord_x * real_part[-1] - coord_y * imag_part[-1]
        new_imag = coord_x * imag_part[-1] + coord_y * real_part[-1]
        real_part.append(new_real)
        imag_part.append(new_imag)
    for azimuthal in range(order_top + 1):
        start_value = (-1.0) ** azimuthal * math.prod(range(2 * azimuthal - 1, 0, -2))
        legendre = {azimuthal: coord_z * 0.0 + start_value}
        if azimuthal + 1 <= degree_top:
            legendre[azimuthal + 1] = coord_z * ((2 * azimuthal + 1) * start_value)
        for degree in range(azimuthal + 2, degree_top + 1):
            legendre[degree] = (
                (2 * degree - 1) * coord_z * legendre[degree - 1]
                - (degree + azimuthal - 1) * legendre[degree - 2]
            ) / (degree - azimuthal)
        for degree in range(azimuthal, degree_top + 1):
            factor = math.sqrt(
                (2 * degree + 1)
                / (4.0 * math.pi)
                * math.factorial(degree - azimuthal)
                / math.factorial(degree + azimuthal)
            )
            if azimuthal == 0:
                results[degree, 0] = factor * legendre[degree]
            else:
                results[degree, azimuthal] = (
                    math.sqrt(2.0) * factor * legendre[degree] * real_part[azimuthal]
                )
                results[degree, -azimuthal] = (
                    math.sqrt(2.0) * factor * legendre[degree] * imag_part[azimuthal]
                )
    return results


def kept_rows():
    row_list = [(degree, 0) for degree in range(LMAX + 1)]
    for azimuthal in range(1, MMAX + 1):
        row_list += [(degree, azimuthal) for degree in range(azimuthal, LMAX + 1)]
        row_list += [(degree, -azimuthal) for degree in range(azimuthal, LMAX + 1)]
    return row_list


def padded_span(degree):
    return -(-(2 * degree + 1) // 8) * 8


def row_offsets():
    listing = []
    offset = 0
    for degree, azimuthal in kept_rows():
        listing.append((degree, offset))
        offset += padded_span(degree)
    return listing


def invert_small(matrix):
    order_size = matrix.shape[0]
    work = np.concatenate([matrix, np.eye(order_size)], axis=1)
    for column in range(order_size):
        work[column] = work[column] / work[column, column]
        for row_index in range(order_size):
            if row_index != column:
                work[row_index] = work[row_index] - work[row_index, column] * work[column]
    return work[:, order_size:]


def sample_tables():
    sample_count = 2 * (LMAX + 1) ** 2
    positions = np.arange(sample_count) + 0.5
    height = 1.0 - 2.0 * positions / sample_count
    radius = np.sqrt(1.0 - height * height)
    azimuth = math.pi * (3.0 - math.sqrt(5.0)) * positions
    points = np.stack([radius * np.cos(azimuth), radius * np.sin(azimuth), height])
    values = harmonics(points[0], points[1], points[2], LMAX, LMAX)
    inverses = []
    for degree in range(LMAX + 1):
        sampled = np.stack([values[degree, azimuthal] for azimuthal in range(-degree, degree + 1)])
        inverses.append(sampled.T @ invert_small(sampled @ sampled.T))
    return (points, inverses)


def wigner_rows(vectors):
    length = jnp.sqrt(jnp.sum(vectors * vectors, axis=0))
    direction = vectors / length
    pick_first = jnp.where(jnp.abs(direction[0]) < 0.6, 1.0, 0.0).astype(jnp.float32)
    helper = jnp.stack([pick_first, 1.0 - pick_first, jnp.zeros_like(pick_first)])
    first_axis = jnp.cross(direction, helper, axis=0)
    first_axis = first_axis / jnp.sqrt(jnp.sum(first_axis * first_axis, axis=0))
    second_axis = jnp.cross(direction, first_axis, axis=0)
    frames = (first_axis, second_axis, direction)
    points, inverses = sample_tables()
    sample = jnp.asarray(points, jnp.float32)
    turned = [
        sum(sample[axis][:, None] * frame[axis][None, :] for axis in range(3)) for frame in frames
    ]
    values = harmonics(turned[0], turned[1], turned[2], LMAX, MMAX)
    edges = vectors.shape[1]
    pieces = {}
    for degree in range(LMAX + 1):
        orders = [row[1] for row in kept_rows() if row[0] == degree]
        stacked = jnp.concatenate([values[degree, order] for order in orders], axis=1)
        span = 2 * degree + 1
        padding = ((0, padded_span(degree) - span), (0, 0))
        table = jnp.asarray(np.pad(inverses[degree].T, padding), jnp.float32)
        product = jnp.dot(table, stacked, precision=lax.Precision.HIGH)
        for index, order in enumerate(orders):
            pieces[degree, order] = product[:, index * edges : (index + 1) * edges]
    envelope = 0.5 * (jnp.cos(math.pi * length / cutoff_radius) + 1.0)
    fade = jnp.broadcast_to(envelope[None, :], (8, edges))
    return jnp.concatenate([pieces[row] for row in kept_rows()] + [fade], axis=0)


def rows_of(degree):
    return [
        (index, offset)
        for index, (row_degree, offset) in enumerate(row_offsets())
        if row_degree == degree
    ]


CHUNK = 32


def forward_kernel(compact_ref, sources_ref, turned_ref, rotation):
    rotation[...] = compact_ref[0].astype(jnp.float32)
    channels = sources_ref.shape[1]

    def body(step, carry):
        span = pl.ds(pl.multiple_of(step * CHUNK, CHUNK), CHUNK)
        for degree in range(LMAX + 1):
            listing = rows_of(degree)
            totals = [None] * len(listing)
            for inner in range(2 * degree + 1):
                value = sources_ref[degree * degree + inner, span, :].astype(jnp.float32)
                for place, (_, offset) in enumerate(listing):
                    at = offset + inner
                    term = rotation[at : at + 1, :] * value
                    totals[place] = term if totals[place] is None else totals[place] + term
            for place, (index, _) in enumerate(listing):
                turned_ref[index, span, :] = totals[place].astype(jnp.bfloat16)
        return carry

    lax.fori_loop(0, channels // CHUNK, body, 0)


def rotate_forward(compact, sources):
    blocks, rows, width = compact.shape
    coefs, channels, edges = sources.shape
    kept = len(kept_rows())
    return pl.pallas_call(
        forward_kernel,
        grid=(blocks,),
        in_specs=[
            pl.BlockSpec((1, rows, width), lambda b: (b, 0, 0)),
            pl.BlockSpec((coefs, channels, width), lambda b: (0, 0, b)),
        ],
        out_specs=pl.BlockSpec((kept, channels, width), lambda b: (0, 0, b)),
        out_shape=jax.ShapeDtypeStruct((kept, channels, edges), jnp.bfloat16),
        scratch_shapes=[pltpu.VMEM((rows, width), jnp.float32)],
        cost_estimate=pl.CostEstimate(
            flops=16_000_000, bytes_accessed=6_000_000, transcendentals=0
        ),
        name="rotate_forward",
    )(compact, sources)


def backward_kernel(starts, compact_ref, scaling_ref, *refs):
    count = len(starts)
    kept_refs, other_refs = refs[:count], refs[count : 2 * count]
    message_ref, rotation = refs[2 * count], refs[2 * count + 1]
    rotation[...] = compact_ref[0].astype(jnp.float32)
    channels = message_ref.shape[1]

    def body(step, carry):
        span = pl.ds(pl.multiple_of(step * CHUNK, CHUNK), CHUNK)
        scale = scaling_ref[0]
        for degree in range(LMAX + 1):
            values = []
            for index, offset in rows_of(degree):
                piece = max(p for p in range(count) if starts[p] <= index)
                row = index - starts[piece]
                mixed = kept_refs[piece][row, span, :].astype(jnp.float32) + other_refs[piece][
                    row, span, :
                ].astype(jnp.float32)
                values.append((mixed * scale, offset))
            for inner in range(2 * degree + 1):
                total = None
                for value, offset in values:
                    at = offset + inner
                    term = rotation[at : at + 1, :] * value
                    total = term if total is None else total + term
                message_ref[degree * degree + inner, span, :] = total.astype(jnp.bfloat16)
        return carry

    lax.fori_loop(0, channels // CHUNK, body, 0)


def rotate_back(compact, scaling, starts, kept, other):
    blocks, rows, width = compact.shape
    _, channels, edges = kept[0].shape
    coefs = (LMAX + 1) ** 2
    part_specs = [
        pl.BlockSpec((part.shape[0], channels, width), lambda b: (0, 0, b)) for part in kept
    ]

    def kernel(*refs):
        backward_kernel(starts, *refs)

    return pl.pallas_call(
        kernel,
        grid=(blocks,),
        in_specs=[
            pl.BlockSpec((1, rows, width), lambda b: (b, 0, 0)),
            pl.BlockSpec((1, 1, width), lambda b: (b, 0, 0)),
        ]
        + part_specs
        + part_specs,
        out_specs=pl.BlockSpec((coefs, channels, width), lambda b: (0, 0, b)),
        out_shape=jax.ShapeDtypeStruct((coefs, channels, edges), jnp.bfloat16),
        scratch_shapes=[pltpu.VMEM((rows, width), jnp.float32)],
        cost_estimate=pl.CostEstimate(
            flops=16_000_000, bytes_accessed=8_000_000, transcendentals=0
        ),
        name="rotate_back",
    )(compact, scaling, *kept, *other)


def mixed_contract(pattern, first_operand, second_operand):
    return jnp.einsum(pattern, first_operand, second_operand, preferred_element_type=jnp.float32)


def exchange(partial, group_count):
    rank = lax.axis_index("chan")
    rows, total, edges = partial.shape
    blocks = partial.reshape(rows, group_count, total // group_count, edges)

    def block(index):
        return lax.dynamic_index_in_dim(blocks, index, 1, keepdims=False)

    def swap(value, bit):
        return lax.ppermute(value, "chan", [(i, i ^ bit) for i in range(group_count)])

    def add(first, second):
        return (first.astype(jnp.float32) + second.astype(jnp.float32)).astype(jnp.bfloat16)

    far, near, far_near = rank ^ 2, rank ^ 1, rank ^ 3
    outgoing = add(block(far), swap(block(far_near), 1))
    arrived = swap(outgoing, 2)
    kept = add(block(rank), swap(block(near), 1))
    return kept, arrived, outgoing


COEFS_PER_STEP = 7


def pick_kernel(index_ref, *refs):
    held_refs, sources_ref = refs[:-1], refs[-1]
    total_nodes = len(held_refs) * held_refs[0].shape[1]
    slab_size = index_ref.shape[1]
    rows = lax.broadcasted_iota(jnp.int32, (total_nodes, slab_size), 0)
    selector = jnp.where(rows == index_ref[...], 1.0, 0.0).astype(jnp.bfloat16)
    for coef in range(COEFS_PER_STEP):
        table = jnp.concatenate([ref[coef] for ref in held_refs], axis=0)
        picked = lax.dot_general(
            table, selector, (((0,), (0,)), ((), ())), preferred_element_type=jnp.float32
        )
        sources_ref[coef] = picked.astype(jnp.bfloat16)


def pick_sources(held, index):
    coefs, nodes, channels = held[0].shape
    slab_size = index.shape[1]
    return pl.pallas_call(
        pick_kernel,
        grid=(coefs // COEFS_PER_STEP,),
        in_specs=[pl.BlockSpec((1, slab_size), lambda k: (0, 0))]
        + [pl.BlockSpec((COEFS_PER_STEP, nodes, channels), lambda k: (k, 0, 0))] * len(held),
        out_specs=pl.BlockSpec((COEFS_PER_STEP, channels, slab_size), lambda k: (k, 0, 0)),
        out_shape=jax.ShapeDtypeStruct((coefs, channels, slab_size), jnp.bfloat16),
        cost_estimate=pl.CostEstimate(
            flops=400_000_000, bytes_accessed=5_000_000, transcendentals=0
        ),
        name="pick_sources",
    )(index, *held)


def shards(
    node_states,
    edge_vectors,
    source_part,
    source_slot,
    target_slot,
    live_edges,
    weight_zero,
    weight_one,
    weight_two,
):
    slab_size = source_slot.shape[0]
    local_nodes = node_states.shape[0]
    local_channels = node_states.shape[2]
    coef_count = node_states.shape[1]
    parts = lax.axis_size("edge")
    groups = lax.axis_size("chan")
    mine = lax.axis_index("edge")
    own = node_states.transpose(1, 0, 2)
    held = [own] + [
        lax.ppermute(own, "edge", [(i, (i + hop) % parts) for i in range(parts)])
        for hop in range(1, parts)
    ]
    compact = lax.all_gather(
        wigner_rows(edge_vectors).astype(jnp.bfloat16), "chan", axis=0, tiled=False
    )
    distance = (mine - source_part[:, 0] + parts) % parts
    sources = pick_sources(held, (distance * local_nodes + source_slot)[None, :])
    turned = rotate_forward(compact, sources)
    sizes = [LMAX + 1, LMAX, LMAX, LMAX - 1, LMAX - 1]
    starts = [sum(sizes[:i]) for i in range(len(sizes))]
    zero, plus_one, minus_one, plus_two, minus_two = [
        turned[start : start + size] for start, size in zip(starts, sizes)
    ]
    pattern = "lce,lcjd->jde"

    def paired(plus, minus, weight):
        first = mixed_contract(pattern, plus, weight[0]) - mixed_contract(pattern, minus, weight[1])
        second = mixed_contract(pattern, minus, weight[0]) + mixed_contract(
            pattern, plus, weight[1]
        )
        return [first, second]

    def spread(partials):
        return [exchange(partial.astype(jnp.bfloat16), groups) for partial in partials]

    summed = spread([mixed_contract(pattern, zero, weight_zero)])
    summed += spread(paired(plus_one, minus_one, weight_one))
    plus_two, minus_two, _ = lax.optimization_barrier((plus_two, minus_two, summed[0][2]))
    summed += spread(paired(plus_two, minus_two, weight_two))
    alive_mask = (jnp.arange(slab_size, dtype=jnp.int32) < live_edges[0]).astype(jnp.float32)
    envelope = compact[:, -1:, :].astype(jnp.float32)
    scaling = envelope * alive_mask.reshape(envelope.shape)
    message = rotate_back(
        compact, scaling, starts, [pair[0] for pair in summed], [pair[1] for pair in summed]
    ).reshape(coef_count * local_channels, slab_size)
    selector = (jnp.arange(local_nodes, dtype=jnp.int32)[:, None] == target_slot[None, :]).astype(
        jnp.bfloat16
    )
    summed = lax.dot_general(
        selector, message, (((1,), (1,)), ((), ())), preferred_element_type=jnp.float32
    )
    return summed.astype(jnp.bfloat16).reshape(local_nodes, coef_count, local_channels)


def solution(mesh):
    in_specs = (
        P("edge", None, "chan"),
        P(None, ("edge", "chan")),
        P("edge", None),
        P("edge"),
        P("edge"),
        P("edge"),
        P(None, "chan", None, None),
        P(None, None, "chan", None, None),
        P(None, None, "chan", None, None),
    )
    out_specs = P("edge", None, "chan")
    return jax.shard_map(shards, mesh=mesh, in_specs=in_specs, out_specs=out_specs, check_vma=False)
```
